32 devices in a mesh: group: 4 (over x, core), tile: 8 (over z, y).
Axes of the slice: x: 2, y: 2, z: 4, core: 2. Of those that a mesh axis runs over, the one named last changes fastest.
Arguments:
- object_slices: bfloat16 [4, 2048, 1024], P(None, 'group', 'tile'), may hold values from -4 to 4
- probe: float32 [1024, 256], replicated, may hold values from -6 to 6
- mid_waves: bfloat16 [4, 8, 3, 2, 2, 256, 256], P('group', 'tile'), may hold values from -160 to 160
- amplitudes: bfloat16 [4, 8, 3, 256, 256], P('group', 'tile'), may hold values from 0.19921875 to 4
- row_offsets: int32 [4, 8, 3], P('group', 'tile'), may hold values from 0 to 256
- col_offsets: int32 [4, 8, 3], P('group', 'tile'), may hold values from 0 to 128
Outputs:
- object_new: float32 [4, 2048, 1024], P(None, 'group', 'tile')
- probe_new: float32 [1024, 256], P('tile')
The draws below stay inside these ranges and needn't reach their ends.
All inputs are finite; a program needn't handle non-finite values.
Results may differ from the reference program's by a relative error of at most 0.0003.
Values may be sent and summed in bfloat16 or wider, within the bound.
No kernel may reach another device: no remote copies, remote signals or barrier semaphores. Data moves between devices by JAX's collectives and lax.ppermute only.
A program may use at most 128 MiB of HBM per device.

```python
import math
import jax
import jax.numpy as jnp
from jax import lax

PX = 256
MODES = 2
POS_DEV = 3
ROWS = 512
COLS_DEV = 128
GROUPS = 4
TILES = 8
NR = 2048
NC = 1024


def draw_mid_waves(key, part):
    shape = (GROUPS, TILES, POS_DEV, 2, MODES, PX, PX)
    total = GROUPS * TILES
    ranking = (jnp.arange(total, dtype=jnp.float32) / max(total - 1, 1)).reshape(GROUPS, TILES, 1, 1, 1, 1, 1)
    values = jnp.clip(jax.random.normal(key, shape, jnp.float32), -5.0, 5.0)
    return (values * (1.0 + 2.0 * ranking)).astype(jnp.bfloat16)


def set_ends(array, key, smallest, high):
    spot = [jax.random.randint(jax.random.fold_in(key, axis), (), 0, length) for axis, length in enumerate(array.shape)]
    widest = array.shape.index(max(array.shape))
    beside = spot[:widest] + [(spot[widest] + 1) % array.shape[widest]] + spot[widest + 1:]
    return array.at[tuple(spot)].set(smallest).at[tuple(beside)].set(high)


def level_of(own_key, dims, shards, smallest, largest):
    loudness = 1.0
    for dim, shards_of in shards:
        draws = jax.random.uniform(jax.random.fold_in(jax.random.fold_in(own_key, 6), dim), (shards_of,), jnp.float32, smallest / len(shards), largest / len(shards))
        loudness = loudness * jnp.repeat(jnp.exp(draws), dims[dim] // shards_of).reshape((-1,) + (1,) * (len(dims) - 1 - dim))
    return loudness


def bell_draw(stream_key, dims, width, bound, pieces=(), kind=jnp.bfloat16):
    drawn = width * jax.random.normal(stream_key, dims, jnp.float32)
    if pieces:
        drawn = drawn * level_of(stream_key, dims, pieces, -0.22, 0.18)
    return jnp.clip(drawn, -bound, bound).astype(kind)


def setup_inputs(seed: int = 0) -> dict:
    splits = jax.random.split(jax.random.key(seed), 7)
    return {
        "object_slices": bell_draw(splits[0], (4, NR, NC), 0.7, 4.0, ((1, 4), (2, 8))),
        "probe": bell_draw(splits[1], (2 * MODES * PX, PX), 1.0, 6.0, (), jnp.float32),
        "mid_waves": draw_mid_waves(jax.random.fold_in(splits[6], 71), 0),
        "amplitudes": jnp.clip(jnp.exp(math.log(4.0) - 2.9996462 * jax.random.uniform(splits[3], (GROUPS, TILES, POS_DEV, PX, PX), jnp.float32) ** level_of(splits[3], (GROUPS, TILES, POS_DEV, PX, PX), ((0, 4), (1, 8)), -0.2, 0.2)), 0.19921875, 4.0).astype(jnp.bfloat16),
        "row_offsets": set_ends(jax.random.randint(splits[4], (GROUPS, TILES, POS_DEV), 0, ROWS - PX + 1), jax.random.fold_in(splits[4], 1), 0, ROWS - PX).astype(jnp.int32),
        "col_offsets": set_ends(jax.random.randint(splits[5], (GROUPS, TILES, POS_DEV), 0, 3 * COLS_DEV - PX + 1), jax.random.fold_in(splits[5], 1), 0, 3 * COLS_DEV - PX).astype(jnp.int32),
    }


phase_rate = 0.25
floor_level = 0.5
object_step = 0.5
probe_step = 0.5
epsilon = 1e-06

def back_kernel():
    freq = jnp.arange(PX, dtype=jnp.int32)
    freq = jnp.where(freq < PX // 2, freq, freq - PX).astype(jnp.float32)
    phase = 2.0 * jnp.pi * phase_rate / PX * (freq[:, None] * freq[:, None] + freq[None, :] * freq[None, :])
    return jnp.cos(phase) + 1j * jnp.sin(phase)

def reference(object_slices, probe, mid_waves, amplitudes, row_offsets, col_offsets):
    obj = object_slices.astype(jnp.float32)
    padded = jnp.pad(obj, ((0, 0), (0, 0), (COLS_DEV, COLS_DEV)))
    probe_parts = probe.reshape(2, MODES, PX, PX)
    probe_cplx = probe_parts[0] + 1j * probe_parts[1]
    kernel = back_kernel()

    def visit(state_sum, device):
        grad_obj, grad_probe = state_sum
        grp = device // TILES
        til = device % TILES
        for position in range(POS_DEV):
            row_at = grp * ROWS + row_offsets[grp, til, position]
            col_at = til * COLS_DEV + col_offsets[grp, til, position]
            patch = lax.dynamic_slice(padded, (jnp.int32(0), row_at, col_at), (4, PX, PX))
            first = patch[0] + 1j * patch[1]
            second = patch[2] + 1j * patch[3]
            wave = mid_waves[grp, til, position].astype(jnp.float32)
            middle = wave[0] + 1j * wave[1]
            amp = amplitudes[grp, til, position].astype(jnp.float32)
            far = jnp.fft.fft2(middle * second[None], norm='ortho')
            power = lax.optimization_barrier(jnp.sum(jnp.real(far) ** 2 + jnp.imag(far) ** 2, axis=0))
            magnitude = jnp.maximum(jnp.sqrt(power), floor_level)
            chi = jnp.fft.ifft2(far * (1.0 - amp / magnitude)[None], norm='ortho')
            grad_second = lax.optimization_barrier(jnp.sum(jnp.conj(middle) * chi, axis=0))
            spectrum = jnp.fft.fft2(jnp.conj(second)[None] * chi, norm='ortho')
            back_wave = jnp.fft.ifft2(spectrum * kernel[None], norm='ortho')
            grad_first = lax.optimization_barrier(jnp.sum(jnp.conj(probe_cplx) * back_wave, axis=0))
            probe_term = jnp.conj(first)[None] * back_wave
            update = jnp.stack([jnp.real(grad_first), jnp.imag(grad_first), jnp.real(grad_second), jnp.imag(grad_second)])
            old = lax.dynamic_slice(grad_obj, (jnp.int32(0), row_at, col_at), (4, PX, PX))
            grad_obj = lax.dynamic_update_slice(grad_obj, old + update, (jnp.int32(0), row_at, col_at))
            grad_probe = grad_probe + jnp.stack([jnp.real(probe_term), jnp.imag(probe_term)])
        return ((grad_obj, grad_probe), None)
    start = (jnp.zeros(padded.shape, jnp.float32), jnp.zeros((2, MODES, PX, PX), jnp.float32))
    (grad_obj, grad_probe), _ = lax.scan(visit, start, jnp.arange(GROUPS * TILES, dtype=jnp.int32))
    grad_obj = grad_obj[:, :, COLS_DEV:COLS_DEV + NC]
    obj_rms = jnp.sqrt(jnp.sum(grad_obj * grad_obj) / (4 * NR * NC) + epsilon)
    object_new = obj - object_step * grad_obj / obj_rms
    grad_probe = grad_probe.reshape(2 * MODES * PX, PX)
    probe_rms = jnp.sqrt(jnp.sum(grad_probe * grad_probe) / (2 * MODES * PX * PX) + epsilon)
    probe_new = probe - probe_step * grad_probe / probe_rms
    return (object_new, probe_new)
```

```python
import jax
import jax.numpy as jnp
import numpy as np
from jax import lax
from jax.experimental import pallas as pl
from jax.experimental.pallas import tpu as pltpu
from jax.sharding import PartitionSpec as P

phase_rate = 0.25
floor_level = 0.5
object_step = 0.5
probe_step = 0.5
epsilon = 1e-06
object_bound = 4.0
amp_bound = 4.0
half_range = 32768.0

F32 = jnp.float32
BF16 = jnp.bfloat16
whole_vmem = pl.BlockSpec(memory_space=pltpu.VMEM)
whole_smem = pl.BlockSpec(memory_space=pltpu.SMEM)


def hi_lo(table):
    table = np.asarray(table, np.float64)
    high = table.astype(np.float32).astype(BF16)
    low = (table - high.astype(np.float64)).astype(np.float32).astype(BF16)
    return np.stack([high, low])


def complex_block(real, imag):
    return np.block([[real, -imag], [imag, real]])


def dft_tables(size):
    half = size // 2
    index = np.arange(half)
    norming = 1.0 / np.sqrt(size)
    tables = []
    for parity in (0, 1):
        angle = 2.0 * np.pi * (np.outer(2 * index + parity, index) % size) / size
        cos, sin = np.cos(angle) * norming, np.sin(angle) * norming
        tables.append(hi_lo(complex_block(cos, -sin)))
        tables.append(hi_lo(complex_block(cos.T, sin.T)))
    left_even, right_even, left_odd, right_odd = tables
    return np.stack([left_even, left_odd, right_even, right_odd])


def back_tables(size):
    half = size // 2
    freq = np.fft.fftfreq(size, 1.0 / size)
    row = np.fft.ifft(np.exp(1j * 2.0 * np.pi * phase_rate / size * freq * freq))
    shift = np.arange(half)[:, None] - np.arange(half)[None, :]
    same, cross = row[shift % size], row[(shift + half) % size]
    even, odd = 0.5 * (same + cross), 0.5 * (same - cross)
    left = [hi_lo(complex_block(part.real, part.imag)) for part in (even, odd)]
    right = [hi_lo(complex_block(part.real, -part.imag)) for part in (even, odd)]
    return np.stack(left + right)


def order_table(size):
    order = np.concatenate([np.arange(0, size, 2), np.arange(1, size, 2)])
    table = np.zeros((size, size), np.float32)
    table[np.arange(size), order] = 1.0
    return np.stack([table, table.T]).astype(BF16)


def dot(left, right):
    return jnp.dot(left, right, preferred_element_type=F32)


def split(value):
    high = value.astype(BF16)
    return high, (value - high.astype(F32)).astype(BF16)


def from_left(table, which, value):
    high, low = split(value)
    return (
        dot(table[which, 0], high) + dot(table[which, 0], low) + dot(table[which, 1], high)
    )


def from_right(value, table, which):
    high, low = split(value)
    return (
        dot(high, table[which, 0]) + dot(low, table[which, 0]) + dot(high, table[which, 1])
    )


def join(parts, axis):
    return jnp.concatenate(parts, axis=axis)


def fold_rows(fields):
    half = fields[0][0].shape[0] // 2
    plus = join([join([part[:half] + part[half:] for part in f], 0) for f in fields], 1)
    minus = join([join([part[:half] - part[half:] for part in f], 0) for f in fields], 1)
    return plus, minus


def fold_lanes(first, second, count):
    half = first.shape[0] // 2
    width = first.shape[1] // count
    plus, minus = [], []
    for mode in range(count):
        for array in (first, second):
            a = array[:, mode * width : mode * width + width // 2]
            b = array[:, mode * width + width // 2 : (mode + 1) * width]
            s, d = a + b, a - b
            plus.append(join([s[:half], s[half:]], 1))
            minus.append(join([d[:half], d[half:]], 1))
    return join(plus, 0), join(minus, 0)


def unfold_lanes(even, odd, count):
    low, high = even + odd, even - odd
    half = even.shape[1] // 2
    arrays = []
    for which in range(2):
        modes = []
        for mode in range(count):
            rows = slice((2 * mode + which) * half, (2 * mode + which + 1) * half)
            x0, x1 = low[rows], high[rows]
            modes.append(
                join([join([x0[:, :half], x1[:, :half]], 1), join([x0[:, half:], x1[:, half:]], 1)], 0)
            )
        arrays.append(join(modes, 1))
    return arrays


def unfold_rows(even, odd, count):
    top, bottom = even + odd, even - odd
    half = even.shape[0] // 2
    width = even.shape[1] // count
    fields = []
    for mode in range(count):
        cols = slice(mode * width, (mode + 1) * width)
        fields.append(
            (
                join([top[:half, cols], bottom[:half, cols]], 0),
                join([top[half:, cols], bottom[half:, cols]], 0),
            )
        )
    return fields


def masks(row_at, col_at, size, width):
    low_rows = lax.broadcasted_iota(jnp.int32, (size, width), 0) >= row_at
    left_cols = lax.broadcasted_iota(jnp.int32, (size, width), 1) >= col_at
    return low_rows, left_cols


def patch_of(left, own, right, part, low_rows, left_cols):
    size = low_rows.shape[0]

    def rows_of(ref):
        return jnp.where(low_rows, ref[part, :size].astype(F32), ref[part, size:].astype(F32))

    halo = jnp.where(left_cols, rows_of(left), rows_of(right))
    return join([halo, rows_of(own)], 1)


def scatter(part, value, scale, left, own, right, low_rows, left_cols):
    size, width = low_rows.shape
    halo, mine = value[:, :width] * scale, value[:, width:]
    zero = jnp.zeros_like(halo)
    to_left = jnp.where(left_cols, halo, zero)
    to_right = halo - to_left
    for ref, term in ((left, to_left), (right, to_right), (own, mine)):
        upper = jnp.where(low_rows, term, zero)
        ref[part, :size] += upper
        ref[part, size:] += term - upper


def prepare_kernel(rows, cols, order, wave, probe, amp, wave_out, probe_out, amp_out, scales, peak):
    position = pl.program_id(0)
    row_at, col_at = rows[position], cols[position]
    parts = wave.shape[1]
    size = wave.shape[2]
    largest = None
    for part in range(parts):
        value = wave[0, part].astype(F32)
        folded = jnp.max(jnp.abs(value), axis=0, keepdims=True)
        largest = folded if largest is None else jnp.maximum(largest, folded)
        wave_out[0, part] = pltpu.roll(pltpu.roll(value, row_at, 0), col_at, 1).astype(BF16)
        value = probe[part * size : (part + 1) * size]
        probe_out[0, part] = pltpu.roll(pltpu.roll(value, row_at, 0), col_at, 1)
    amp_out[0] = dot(dot(order[0], amp[0]).astype(BF16), order[1]).astype(BF16)

    @pl.when(position == 0)
    def _():
        peak[...] = jnp.zeros_like(peak)

    peak[0:1] = jnp.maximum(peak[0:1], largest)

    @pl.when(position == pl.num_programs(0) - 1)
    def _():
        count = pl.num_programs(0) * (parts // 2)
        wave_peak = jnp.max(peak[0:1])
        probe_peak = jnp.max(jnp.abs(probe[...]))
        root = 2.0**0.5
        chi_bound = size * (2.0 * object_bound * wave_peak + amp_bound)
        second = count * root * wave_peak * chi_bound
        first = count * root * probe_peak * (root * object_bound * chi_bound)
        tile = lax.broadcasted_iota(jnp.int32, scales.shape, 0)
        scales[...] = jnp.maximum(jnp.where(tile < 4, second, first), 1e-30) * (1.0 / half_range)


def clear(refs):
    @pl.when(pl.program_id(0) == 0)
    def _():
        for ref in refs:
            ref[...] = jnp.zeros_like(ref)


def exit_kernel(rows, cols, tables, left_in, own_in, right_in, scales, wave, amp, back, left, own, right):
    position = pl.program_id(0)
    size = wave.shape[2]
    width = own_in.shape[2]
    half = size // 2
    count = wave.shape[1] // 2
    clear((left, own, right))
    low_rows, left_cols = masks(rows[position], cols[position], size, width)
    second_real = patch_of(left_in, own_in, right_in, 0, low_rows, left_cols)
    second_imag = patch_of(left_in, own_in, right_in, 1, low_rows, left_cols)
    fields = []
    for mode in range(count):
        mid_real, mid_imag = wave[0, mode].astype(F32), wave[0, count + mode].astype(F32)
        fields.append(
            (
                mid_real * second_real - mid_imag * second_imag,
                mid_real * second_imag + mid_imag * second_real,
            )
        )
    plus, minus = fold_rows(fields)
    plus, minus = fold_lanes(from_left(tables, 0, plus), from_left(tables, 1, minus), count)
    spectra = [from_right(plus, tables, 2), from_right(minus, tables, 3)]
    filtered = []
    for lane, spectrum in enumerate(spectra):
        rows_of = []
        for row in range(2):
            power = None
            for mode in range(count):
                block = spectrum[(2 * mode + row) * half : (2 * mode + row + 1) * half]
                squares = block[:, :half] * block[:, :half] + block[:, half:] * block[:, half:]
                power = squares if power is None else power + squares
            level = amp[0, row * half : (row + 1) * half, lane * half : (lane + 1) * half]
            factor = 1.0 - level.astype(F32) * jnp.minimum(lax.rsqrt(power), 1.0 / floor_level)
            rows_of.append(join([factor, factor], 1))
        filtered.append(spectrum * join(rows_of * count, 0))
    evens, odds = unfold_lanes(
        from_right(filtered[0], tables, 0), from_right(filtered[1], tables, 1), count
    )
    fields = unfold_rows(from_left(tables, 2, evens), from_left(tables, 3, odds), count)
    grad_real = grad_imag = None
    for mode, (chi_real, chi_imag) in enumerate(fields):
        mid_real, mid_imag = wave[0, mode].astype(F32), wave[0, count + mode].astype(F32)
        real = mid_real * chi_real + mid_imag * chi_imag
        imag = mid_real * chi_imag - mid_imag * chi_real
        grad_real = real if grad_real is None else grad_real + real
        grad_imag = imag if grad_imag is None else grad_imag + imag
        back[0, mode] = second_real * chi_real + second_imag * chi_imag
        back[0, count + mode] = second_real * chi_imag - second_imag * chi_real
    inverse = 1.0 / scales[0:1, :width]
    scatter(0, grad_real, inverse, left, own, right, low_rows, left_cols)
    scatter(1, grad_imag, inverse, left, own, right, low_rows, left_cols)


def back_kernel(rows, cols, tables, scales, back, probe, wave, left, own, right):
    position = pl.program_id(0)
    size = back.shape[2]
    width = own.shape[2]
    count = back.shape[1] // 2
    clear((left, own, right))
    low_rows, left_cols = masks(rows[position], cols[position], size, width)
    fields = [(back[0, mode], back[0, count + mode]) for mode in range(count)]
    plus, minus = fold_rows(fields)
    even, odd = from_left(tables, 0, plus), from_left(tables, 1, minus)
    plus, minus = fold_lanes(even + odd, even - odd, count)
    top, bottom = unfold_lanes(
        from_right(plus, tables, 2), from_right(minus, tables, 3), count
    )
    half = size // 2
    grad_real = grad_imag = None
    for mode in range(count):
        lanes = slice(mode * size, (mode + 1) * size)
        real = join([top[:half, lanes], bottom[:half, lanes]], 0)
        imag = join([top[half:, lanes], bottom[half:, lanes]], 0)
        wave[0, mode] = real
        wave[0, count + mode] = imag
        probe_real, probe_imag = probe[0, mode], probe[0, count + mode]
        term_real = probe_real * real + probe_imag * imag
        term_imag = probe_real * imag - probe_imag * real
        grad_real = term_real if grad_real is None else grad_real + term_real
        grad_imag = term_imag if grad_imag is None else grad_imag + term_imag
    inverse = 1.0 / scales[4:5, :width]
    scatter(0, grad_real, inverse, left, own, right, low_rows, left_cols)
    scatter(1, grad_imag, inverse, left, own, right, low_rows, left_cols)


def probe_kernel(rows, cols, left_in, own_in, right_in, wave, grad):
    position = pl.program_id(0)
    size = wave.shape[2]
    width = own_in.shape[2]
    count = wave.shape[1] // 2
    clear((grad,))
    row_at, col_at = rows[position], cols[position]
    low_rows, left_cols = masks(row_at, col_at, size, width)
    real = patch_of(left_in, own_in, right_in, 0, low_rows, left_cols)
    imag = patch_of(left_in, own_in, right_in, 1, low_rows, left_cols)
    row_back, col_back = size - row_at, size - col_at
    for mode in range(count):
        wave_real, wave_imag = wave[0, mode], wave[0, count + mode]
        for part, value in (
            (mode, real * wave_real + imag * wave_imag),
            (count + mode, real * wave_imag - imag * wave_real),
        ):
            value = pltpu.roll(pltpu.roll(value, row_back, 0), col_back, 1)
            grad[part * size : (part + 1) * size] += value


def shape_of(shape, kind=F32):
    return jax.ShapeDtypeStruct(shape, kind)


def block_of(shape):
    rest = (0,) * (len(shape) - 1)
    return pl.BlockSpec((1,) + tuple(shape[1:]), lambda p, *_: (p,) + rest)


def fixed(shape):
    zeros = (0,) * len(shape)
    return pl.BlockSpec(tuple(shape), lambda p, *_: zeros)


def call(kernel, count, ins, outs, scratch=(), flops=0, transcendentals=0):
    moved = sum(int(np.prod(a.shape)) * a.dtype.itemsize for a, _ in ins + outs)
    return pl.pallas_call(
        kernel,
        grid_spec=pltpu.PrefetchScalarGridSpec(
            num_scalar_prefetch=2,
            grid=(count,),
            in_specs=[block_of(a.shape) if cut else fixed(a.shape) for a, cut in ins[2:]],
            out_specs=[block_of(a.shape) if cut else fixed(a.shape) for a, cut in outs],
            scratch_shapes=list(scratch),
        ),
        out_shape=[a for a, _ in outs],
        cost_estimate=pl.CostEstimate(
            flops=flops, bytes_accessed=moved, transcendentals=transcendentals
        ),
        compiler_params=pltpu.CompilerParams(
            dimension_semantics=("arbitrary",), vmem_limit_bytes=48 * 1024 * 1024
        ),
    )(*[a for a, _ in ins])


def shifted(block, axis, distance):
    devices = range(lax.axis_size(axis))
    route = [(i - distance, i) for i in devices if i - distance in devices]
    return lax.ppermute(block, axis, route)


def swapped(block, axis, bit):
    return lax.ppermute(block, axis, [(i, i ^ bit) for i in range(lax.axis_size(axis))])


def halved_sum(block, dim, axis, bit, low):
    mine = (lax.axis_index(axis) // bit) % 2
    half = block.shape[dim] // 2
    pair = (half, 2) if low else (2, half)
    view = block.reshape(block.shape[:dim] + pair + block.shape[dim + 1 :])
    at = dim + 1 if low else dim
    keep = lax.dynamic_index_in_dim(view, mine, at, False)
    send = lax.dynamic_index_in_dim(view, 1 - mine, at, False)
    return keep + swapped(send, axis, bit)


def bits_of(axis):
    bit = lax.axis_size(axis) // 2
    bits = []
    while bit:
        bits.append(bit)
        bit //= 2
    return bits


def summed(values):
    axes = ("group", "tile")
    count = lax.axis_size("group") * lax.axis_size("tile")
    copies = jnp.broadcast_to(values[None], (count,) + values.shape)
    return jnp.sum(lax.all_to_all(copies, axes, 0, 0, tiled=True), axis=0)


def shards(object_slices, probe, mid_waves, amplitudes, row_offsets, col_offsets):
    row_count, strip_width = object_slices.shape[1:]
    size = probe.shape[1]
    count = mid_waves.shape[2]
    modes = probe.shape[0] // (2 * size)
    assert row_count == 2 * size and size == 2 * strip_width and size % 256 == 0
    groups, tiles = lax.axis_size("group"), lax.axis_size("tile")
    rows, cols = row_offsets.reshape(count), col_offsets.reshape(count)
    waves = mid_waves.reshape(count, 2 * modes, size, size)
    levels = amplitudes.reshape(count, size, size)
    first, second = object_slices[:2], object_slices[2:]
    left_second, right_second = shifted(second, "tile", 1), shifted(second, "tile", -1)
    left_first, right_first = shifted(first, "tile", 1), shifted(first, "tile", -1)

    planes = (count, 2 * modes, size, size)
    product = 2 * size**3
    rolled_waves, rolled_probe, ordered, scales = call(
        prepare_kernel,
        count,
        [
            (rows, 0),
            (cols, 0),
            (jnp.asarray(order_table(size)), 0),
            (waves, 1),
            (probe, 0),
            (levels, 1),
        ],
        [
            (shape_of(planes, BF16), 1),
            (shape_of(planes), 1),
            (shape_of(levels.shape, BF16), 1),
            (shape_of((8, strip_width)), 0),
        ],
        scratch=[pltpu.VMEM((8, size), F32)],
        flops=count * 2 * product,
    )
    left_scales, right_scales = shifted(scales, "tile", 1), shifted(scales, "tile", -1)
    rim = shape_of((2, row_count, strip_width))
    back, left_rim, own_second, right_rim = call(
        exit_kernel,
        count,
        [
            (rows, 0),
            (cols, 0),
            (jnp.asarray(dft_tables(size)), 0),
            (left_second, 0),
            (second, 0),
            (right_second, 0),
            (scales, 0),
            (rolled_waves, 1),
            (ordered, 1),
        ],
        [(shape_of(planes), 1), (rim, 0), (rim, 0), (rim, 0)],
        flops=count * modes * 24 * product,
    )
    from_right_second = shifted(left_rim.astype(jnp.float16), "tile", -1)
    from_left_second = shifted(right_rim.astype(jnp.float16), "tile", 1)
    waves_back, left_rim, own_first, right_rim = call(
        back_kernel,
        count,
        [
            (rows, 0),
            (cols, 0),
            (jnp.asarray(back_tables(size)), 0),
            (scales, 0),
            (back, 1),
            (rolled_probe, 1),
        ],
        [(shape_of(planes), 1), (rim, 0), (rim, 0), (rim, 0)],
        flops=count * modes * 12 * product,
    )
    from_right_first = shifted(left_rim.astype(jnp.float16), "tile", -1)
    from_left_first = shifted(right_rim.astype(jnp.float16), "tile", 1)
    (grad_probe,) = call(
        probe_kernel,
        count,
        [
            (rows, 0),
            (cols, 0),
            (left_first, 0),
            (first, 0),
            (right_first, 0),
            (waves_back, 1),
        ],
        [(shape_of(probe.shape), 0)],
        flops=count * 8 * modes * size * size,
    )

    share = probe.shape[0] // tiles
    piece = share // groups
    part = grad_probe.reshape(tiles, groups, piece, size)
    for bit in reversed(bits_of("group")):
        part = halved_sum(part, 1, "group", bit, True)
    for bit in bits_of("tile"):
        part = halved_sum(part, 0, "tile", bit, False)
    part = part.reshape(piece, size)
    probe_squares = jnp.sum(part * part)

    own_second = (
        own_second
        + from_right_second.astype(F32) * right_scales[0, 0]
        + from_left_second.astype(F32) * left_scales[0, 0]
    )
    own_first = (
        own_first
        + from_right_first.astype(F32) * right_scales[4, 0]
        + from_left_first.astype(F32) * left_scales[4, 0]
    )
    own_grad = jnp.concatenate([own_first, own_second])
    object_squares = jnp.sum(own_grad * own_grad)
    object_total = summed(object_squares.reshape(1))[0]
    probe_total = summed(probe_squares.reshape(1))[0]
    object_count = 4 * row_count * strip_width * groups * tiles
    object_rms = jnp.sqrt(object_total / object_count + epsilon)
    object_new = object_slices.astype(F32) - object_step * own_grad / object_rms

    whole = part
    for bit in reversed(bits_of("group")):
        other = swapped(whole, "group", bit)
        mine = (lax.axis_index("group") // bit) % 2
        whole = jnp.where(
            mine == 0,
            jnp.concatenate([whole, other]),
            jnp.concatenate([other, whole]),
        )
    probe_rms = jnp.sqrt(probe_total / probe.size + epsilon)
    start_row = lax.axis_index("tile") * share
    probe_rows = lax.dynamic_slice_in_dim(probe, start_row, share, 0)
    probe_new = probe_rows - probe_step * whole / probe_rms
    return (object_new, probe_new)


def solution(mesh):
    return jax.shard_map(
        shards,
        mesh=mesh,
        in_specs=(
            P(None, "group", "tile"),
            P(),
            P("group", "tile", None, None, None, None, None),
            P("group", "tile", None, None, None),
            P("group", "tile", None),
            P("group", "tile", None),
        ),
        out_specs=(P(None, "group", "tile"), P("tile", None)),
        check_vma=False,
    )
```

```python
import jax
import jax.numpy as jnp
import numpy as np
from jax import lax
from jax.experimental import pallas as pl
from jax.experimental.pallas import tpu as pltpu
from jax.sharding import PartitionSpec as P


phase_rate = 0.25
floor_level = 0.5
object_step = 0.5
probe_step = 0.5
epsilon = 1e-06
object_bound = 4.0
amp_bound = 4.0
half_range = 32768.0
vmem_part = 22 * 1024 * 1024
prep_far = (0, 1, 2, 3, 4, 5, 6)
exit_far = (0, 1, 2, 3, 5, 8)
back_far = (0, 1, 2, 6)
grad_far = (0, 1)

F32 = jnp.float32
BF16 = jnp.bfloat16
whole_vmem = pl.BlockSpec(memory_space=pltpu.VMEM)
whole_smem = pl.BlockSpec(memory_space=pltpu.SMEM)


def hi_lo(table):
    table = np.asarray(table, np.float64)
    high = table.astype(np.float32).astype(BF16)
    low = (table - high.astype(np.float64)).astype(np.float32).astype(BF16)
    return np.stack([high, low])


def complex_block(real, imag):
    return np.block([[real, -imag], [imag, real]])


def dft_tables(size):
    half = size // 2
    index = np.arange(half)
    norming = 1.0 / np.sqrt(size)
    tables = []
    for parity in (0, 1):
        angle = 2.0 * np.pi * (np.outer(2 * index + parity, index) % size) / size
        cos, sin = np.cos(angle) * norming, np.sin(angle) * norming
        tables.append(hi_lo(complex_block(cos, -sin)))
        tables.append(hi_lo(complex_block(cos.T, sin.T)))
    left_even, right_even, left_odd, right_odd = tables
    return np.stack([left_even, left_odd, right_even, right_odd])


def back_tables(size):
    half = size // 2
    freq = np.fft.fftfreq(size, 1.0 / size)
    row = np.fft.ifft(np.exp(1j * 2.0 * np.pi * phase_rate / size * freq * freq))
    shift = np.arange(half)[:, None] - np.arange(half)[None, :]
    same, cross = row[shift % size], row[(shift + half) % size]
    even, odd = 0.5 * (same + cross), 0.5 * (same - cross)
    left = [hi_lo(complex_block(part.real, part.imag)) for part in (even, odd)]
    right = [hi_lo(complex_block(part.real, -part.imag)) for part in (even, odd)]
    return np.stack(left + right)


def order_table(size):
    order = np.concatenate([np.arange(0, size, 2), np.arange(1, size, 2)])
    table = np.zeros((size, size), np.float32)
    table[np.arange(size), order] = 1.0
    return np.stack([table, table.T]).astype(BF16)


def dot(left, right):
    return jnp.dot(left, right, preferred_element_type=F32)


def split(value):
    high = value.astype(BF16)
    return high, (value - high.astype(F32)).astype(BF16)


def from_left(table, which, value):
    high, low = split(value)
    return (
        dot(table[which, 0], high) + dot(table[which, 0], low) + dot(table[which, 1], high)
    )


def from_right(value, table, which):
    high, low = split(value)
    return (
        dot(high, table[which, 0]) + dot(low, table[which, 0]) + dot(high, table[which, 1])
    )


def join(parts, axis):
    return jnp.concatenate(parts, axis=axis)


def fold_rows(fields):
    half = fields[0][0].shape[0] // 2
    plus = join([join([part[:half] + part[half:] for part in f], 0) for f in fields], 1)
    minus = join([join([part[:half] - part[half:] for part in f], 0) for f in fields], 1)
    return plus, minus


def fold_lanes(first, second, count):
    half = first.shape[0] // 2
    width = first.shape[1] // count
    plus, minus = [], []
    for mode in range(count):
        for array in (first, second):
            a = array[:, mode * width : mode * width + width // 2]
            b = array[:, mode * width + width // 2 : (mode + 1) * width]
            s, d = a + b, a - b
            plus.append(join([s[:half], s[half:]], 1))
            minus.append(join([d[:half], d[half:]], 1))
    return join(plus, 0), join(minus, 0)


def unfold_lanes(even, odd, count):
    low, high = even + odd, even - odd
    half = even.shape[1] // 2
    arrays = []
    for which in range(2):
        modes = []
        for mode in range(count):
            rows = slice((2 * mode + which) * half, (2 * mode + which + 1) * half)
            x0, x1 = low[rows], high[rows]
            modes.append(
                join([join([x0[:, :half], x1[:, :half]], 1), join([x0[:, half:], x1[:, half:]], 1)], 0)
            )
        arrays.append(join(modes, 1))
    return arrays


def unfold_rows(even, odd, count):
    top, bottom = even + odd, even - odd
    half = even.shape[0] // 2
    width = even.shape[1] // count
    fields = []
    for mode in range(count):
        cols = slice(mode * width, (mode + 1) * width)
        fields.append(
            (
                join([top[:half, cols], bottom[:half, cols]], 0),
                join([top[half:, cols], bottom[half:, cols]], 0),
            )
        )
    return fields


def masks(row_at, col_at, size, width):
    low_rows = lax.broadcasted_iota(jnp.int32, (size, width), 0) >= row_at
    left_cols = lax.broadcasted_iota(jnp.int32, (size, width), 1) >= col_at
    return low_rows, left_cols


def patch_of(left, own, right, part, low_rows, left_cols):
    size = low_rows.shape[0]

    def rows_of(ref):
        return jnp.where(low_rows, ref[part, :size].astype(F32), ref[part, size : 2 * size].astype(F32))

    halo = jnp.where(left_cols, rows_of(left), rows_of(right))
    return join([halo, rows_of(own)], 1)


def scatter(part, value, scale, left, own, right, low_rows, left_cols):
    size, width = low_rows.shape
    halo, mine = value[:, :width] * scale, value[:, width:]
    zero = jnp.zeros_like(halo)
    to_left = jnp.where(left_cols, halo, zero)
    to_right = halo - to_left
    for ref, term in ((left, to_left), (right, to_right), (own, mine)):
        upper = jnp.where(low_rows, term, zero)
        ref[part, :size] += upper
        ref[part, size : 2 * size] += term - upper


def prepare_kernel(
    rows, cols, order, wave, probe, amp, strip, wave_out, probe_out, amp_out, first_out, exponents, peak
):
    position = pl.program_id(0)
    row_at, col_at = rows[position], cols[position]
    parts = wave.shape[1]
    size = wave.shape[2]
    largest = None
    for part in range(parts):
        value = wave[0, part].astype(F32)
        folded = jnp.max(jnp.abs(value), axis=0, keepdims=True)
        largest = folded if largest is None else jnp.maximum(largest, folded)
        wave_out[0, part] = pltpu.roll(pltpu.roll(value, row_at, 0), col_at, 1).astype(BF16)
        value = probe[part * size : (part + 1) * size]
        probe_out[0, part] = pltpu.roll(pltpu.roll(value, row_at, 0), col_at, 1)
    amp_out[0] = dot(dot(order[0], amp[0]).astype(BF16), order[1]).astype(BF16)

    @pl.when(position == 0)
    def _():
        peak[...] = jnp.zeros_like(peak)
        first_out[...] = strip[:2]

    peak[0:1] = jnp.maximum(peak[0:1], largest)

    @pl.when(position == pl.num_programs(0) - 1)
    def _():
        count = pl.num_programs(0) * (parts // 2)
        wave_peak = jnp.max(peak[0:1])
        probe_peak = jnp.max(jnp.abs(probe[...]))
        root = 2.0**0.5
        chi_bound = size * (2.0 * object_bound * wave_peak + amp_bound)
        second = count * root * wave_peak * chi_bound
        first = count * root * probe_peak * (root * object_bound * chi_bound)
        shared = count * root * object_bound * (root * object_bound * chi_bound)
        row = lax.broadcasted_iota(jnp.int32, exponents.shape, 0)
        bound = jnp.where(row < 8, second, jnp.where(row < 16, first, shared))
        bound = jnp.maximum(bound, 1e-30)
        exponents[...] = jnp.ceil(jnp.log2(bound * (1.0 / half_range)))


def clear(refs):
    @pl.when(pl.program_id(0) == 0)
    def _():
        for ref in refs:
            ref[...] = jnp.zeros_like(ref)


def exit_kernel(rows, cols, tables, left_in, own_in, right_in, exponents, wave, amp, back, left, own, right):
    position = pl.program_id(0)
    size = wave.shape[2]
    width = own_in.shape[2]
    half = size // 2
    count = wave.shape[1] // 2
    clear((left, own, right))
    left[:, 2 * size :] = jnp.broadcast_to(exponents[:16], (2, 16, width))
    low_rows, left_cols = masks(rows[position], cols[position], size, width)
    second_real = patch_of(left_in, own_in, right_in, 0, low_rows, left_cols)
    second_imag = patch_of(left_in, own_in, right_in, 1, low_rows, left_cols)
    fields = []
    for mode in range(count):
        mid_real, mid_imag = wave[0, mode].astype(F32), wave[0, count + mode].astype(F32)
        fields.append(
            (
                mid_real * second_real - mid_imag * second_imag,
                mid_real * second_imag + mid_imag * second_real,
            )
        )
    plus, minus = fold_rows(fields)
    plus, minus = fold_lanes(from_left(tables, 0, plus), from_left(tables, 1, minus), count)
    spectra = [from_right(plus, tables, 2), from_right(minus, tables, 3)]
    filtered = []
    for lane, spectrum in enumerate(spectra):
        rows_of = []
        for row in range(2):
            power = None
            for mode in range(count):
                block = spectrum[(2 * mode + row) * half : (2 * mode + row + 1) * half]
                squares = block[:, :half] * block[:, :half] + block[:, half:] * block[:, half:]
                power = squares if power is None else power + squares
            level = amp[0, row * half : (row + 1) * half, lane * half : (lane + 1) * half]
            factor = 1.0 - level.astype(F32) * jnp.minimum(lax.rsqrt(power), 1.0 / floor_level)
            rows_of.append(join([factor, factor], 1))
        filtered.append(spectrum * join(rows_of * count, 0))
    evens, odds = unfold_lanes(
        from_right(filtered[0], tables, 0), from_right(filtered[1], tables, 1), count
    )
    fields = unfold_rows(from_left(tables, 2, evens), from_left(tables, 3, odds), count)
    grad_real = grad_imag = None
    for mode, (chi_real, chi_imag) in enumerate(fields):
        mid_real, mid_imag = wave[0, mode].astype(F32), wave[0, count + mode].astype(F32)
        real = mid_real * chi_real + mid_imag * chi_imag
        imag = mid_real * chi_imag - mid_imag * chi_real
        grad_real = real if grad_real is None else grad_real + real
        grad_imag = imag if grad_imag is None else grad_imag + imag
        back[0, mode] = second_real * chi_real + second_imag * chi_imag
        back[0, count + mode] = second_real * chi_imag - second_imag * chi_real
    inverse = jnp.exp2(-exponents[0:1])
    scatter(0, grad_real, inverse, left, own, right, low_rows, left_cols)
    scatter(1, grad_imag, inverse, left, own, right, low_rows, left_cols)


def back_kernel(
    rows, cols, tables, exponents, right_second, back, probe, wave, left, own, right
):
    position = pl.program_id(0)
    size = back.shape[2]
    width = own.shape[2]
    count = back.shape[1] // 2
    clear((left, own))

    @pl.when(position == 0)
    def _():
        right[:2, : 2 * size] = jnp.zeros((2, 2 * size, width), F32)
        right[2:, : 2 * size] = right_second[...]
        right[:, 2 * size :] = jnp.broadcast_to(exponents[:16], (4, 16, width))

    low_rows, left_cols = masks(rows[position], cols[position], size, width)
    fields = [(back[0, mode], back[0, count + mode]) for mode in range(count)]
    plus, minus = fold_rows(fields)
    even, odd = from_left(tables, 0, plus), from_left(tables, 1, minus)
    plus, minus = fold_lanes(even + odd, even - odd, count)
    top, bottom = unfold_lanes(
        from_right(plus, tables, 2), from_right(minus, tables, 3), count
    )
    half = size // 2
    grad_real = grad_imag = None
    for mode in range(count):
        lanes = slice(mode * size, (mode + 1) * size)
        real = join([top[:half, lanes], bottom[:half, lanes]], 0)
        imag = join([top[half:, lanes], bottom[half:, lanes]], 0)
        wave[0, mode] = real
        wave[0, count + mode] = imag
        probe_real, probe_imag = probe[0, mode], probe[0, count + mode]
        term_real = probe_real * real + probe_imag * imag
        term_imag = probe_real * imag - probe_imag * real
        grad_real = term_real if grad_real is None else grad_real + term_real
        grad_imag = term_imag if grad_imag is None else grad_imag + term_imag
    inverse = jnp.exp2(-exponents[8:9])
    scatter(0, grad_real, inverse, left, own, right, low_rows, left_cols)
    scatter(1, grad_imag, inverse, left, own, right, low_rows, left_cols)


def probe_kernel(rows, cols, left_in, own_in, right_in, wave, grad):
    position = pl.program_id(0)
    size = wave.shape[2]
    width = own_in.shape[2]
    count = wave.shape[1] // 2
    clear((grad,))
    row_at, col_at = rows[position], cols[position]
    low_rows, left_cols = masks(row_at, col_at, size, width)
    real = patch_of(left_in, own_in, right_in, 0, low_rows, left_cols)
    imag = patch_of(left_in, own_in, right_in, 1, low_rows, left_cols)
    row_back, col_back = size - row_at, size - col_at
    for mode in range(count):
        wave_real, wave_imag = wave[0, mode], wave[0, count + mode]
        for part, value in (
            (mode, real * wave_real + imag * wave_imag),
            (count + mode, real * wave_imag - imag * wave_real),
        ):
            value = pltpu.roll(pltpu.roll(value, row_back, 0), col_back, 1)
            grad[part * size : (part + 1) * size] += value


def shape_of(shape, kind=F32):
    return jax.ShapeDtypeStruct(shape, kind)


def block_of(shape):
    rest = (0,) * (len(shape) - 1)
    return pl.BlockSpec((1,) + tuple(shape[1:]), lambda p, *_: (p,) + rest)


def fixed(shape):
    zeros = (0,) * len(shape)
    return pl.BlockSpec(tuple(shape), lambda p, *_: zeros)


def call(kernel, count, ins, outs, flops, limit=None, scratch=(), far=(), near=(), kept=(), shed=()):
    moved = sum(int(np.prod(a.shape)) * a.dtype.itemsize for a, _ in ins + outs)
    given = [a for a, _ in ins]
    for places, space in ((far, pltpu.HBM), (near, pltpu.VMEM)):
        for at in places:
            given[at] = pltpu.with_memory_space_constraint(given[at], space)
    return pl.pallas_call(
        kernel,
        grid_spec=pltpu.PrefetchScalarGridSpec(
            num_scalar_prefetch=2,
            grid=(count,),
            in_specs=[block_of(a.shape) if cut else fixed(a.shape) for a, cut in ins[2:]],
            out_specs=[block_of(a.shape) if cut else fixed(a.shape) for a, cut in outs],
            scratch_shapes=list(scratch),
        ),
        out_shape=[
            pltpu.VMEM(a.shape, a.dtype)
            if at in kept
            else pltpu.HBM(a.shape, a.dtype)
            if at in shed
            else a
            for at, (a, _) in enumerate(outs)
        ],
        cost_estimate=pl.CostEstimate(flops=flops, bytes_accessed=moved, transcendentals=0),
        compiler_params=pltpu.CompilerParams(
            dimension_semantics=("arbitrary",), vmem_limit_bytes=limit or vmem_part
        ),
    )(*given)


def shifted(block, axis, distance):
    devices = range(lax.axis_size(axis))
    route = [(i - distance, i) for i in devices if i - distance in devices]
    return lax.ppermute(block, axis, route)


def swapped(block, axis, bit):
    return lax.ppermute(block, axis, [(i, i ^ bit) for i in range(lax.axis_size(axis))])


def summed(values):
    axes = ("group", "tile")
    count = lax.axis_size("group") * lax.axis_size("tile")
    copies = jnp.broadcast_to(values[None], (count,) + values.shape)
    return jnp.sum(lax.all_to_all(copies, axes, 0, 0, tiled=True), axis=0)


def lane_row(values):
    lane = lax.broadcasted_iota(jnp.int32, (128,), 0)
    row = jnp.zeros((128,), F32)
    for at, value in enumerate(values):
        row = jnp.where(lane == at, value, row)
    return row


def shards(object_slices, probe, mid_waves, amplitudes, row_offsets, col_offsets):
    row_count, strip_width = object_slices.shape[1:]
    size = probe.shape[1]
    count = mid_waves.shape[2]
    modes = probe.shape[0] // (2 * size)
    assert row_count == 2 * size and size == 2 * strip_width and size % 256 == 0
    groups, tiles = lax.axis_size("group"), lax.axis_size("tile")
    rows, cols = row_offsets.reshape(count), col_offsets.reshape(count)
    waves = mid_waves.reshape(count, 2 * modes, size, size)
    levels = amplitudes.reshape(count, size, size)
    second = object_slices[2:]
    left_second = shifted(second, "tile", 1)
    right_second = shifted(second, "tile", -1)

    planes = (count, 2 * modes, size, size)
    product = 2 * size**3
    rolled_waves, rolled_probe, ordered, first, exponents = call(
        prepare_kernel,
        count,
        [
            (rows, 0),
            (cols, 0),
            (jnp.asarray(order_table(size)), 0),
            (waves, 1),
            (probe, 0),
            (levels, 1),
            (object_slices, 0),
        ],
        [
            (shape_of(planes, BF16), 1),
            (shape_of(planes), 1),
            (shape_of(levels.shape, BF16), 1),
            (shape_of(second.shape, BF16), 0),
            (shape_of((24, strip_width)), 0),
        ],
        scratch=[pltpu.VMEM((8, size), F32)],
        far=prep_far,
        kept=(0, 4),
        shed=(1, 2),
        flops=count * 2 * product,
    )
    left_first_strip = shifted(first, "tile", 1)
    right_first_strip = shifted(first, "tile", -1)
    strip = shape_of((2, row_count, strip_width))
    tailed = row_count + 16
    back, left_rim, own_second, right_second = call(
        exit_kernel,
        count,
        [
            (rows, 0),
            (cols, 0),
            (jnp.asarray(dft_tables(size)), 0),
            (left_second, 0),
            (second, 0),
            (right_second, 0),
            (exponents, 0),
            (rolled_waves, 1),
            (ordered, 1),
        ],
        [(shape_of(planes), 1), (shape_of((2, tailed, strip_width)), 0), (strip, 0), (strip, 0)],
        flops=count * modes * 24 * product,
        far=exit_far,
        near=(6, 7),
        kept=(0, 1, 2, 3),
    )
    second_from_right = shifted(left_rim.astype(jnp.float16), "tile", -1)
    beams, left_first, own_first, right_rim = call(
        back_kernel,
        count,
        [
            (rows, 0),
            (cols, 0),
            (jnp.asarray(back_tables(size)), 0),
            (exponents, 0),
            (right_second, 0),
            (back, 1),
            (rolled_probe, 1),
        ],
        [(shape_of(planes), 1), (strip, 0), (strip, 0), (shape_of((4, tailed, strip_width)), 0)],
        flops=count * modes * 12 * product,
        far=back_far,
        near=(3, 4, 5),
        kept=(0, 1, 2, 3),
    )
    from_left = shifted(right_rim.astype(jnp.float16), "tile", 1)
    first_from_right = shifted(left_first.astype(jnp.float16), "tile", -1)
    (grad_probe,) = call(
        probe_kernel,
        count,
        [
            (rows, 0),
            (cols, 0),
            (left_first_strip, 0),
            (first, 0),
            (right_first_strip, 0),
            (beams, 1),
        ],
        [(shape_of(probe.shape), 0)],
        flops=count * 8 * modes * size * size,
        far=grad_far,
        near=(5,),
        kept=(0,),
    )

    share = probe.shape[0] // tiles
    piece = share // groups
    chips = groups // 2
    core = lax.axis_index("group") % 2
    view = grad_probe.reshape(tiles, chips, 2, piece, size)
    keep = lax.dynamic_index_in_dim(view, core, 2, False)
    send = lax.dynamic_index_in_dim(view, 1 - core, 2, False)
    part = (keep + swapped(send, "group", 1)).swapaxes(0, 1)
    lines = piece * size // strip_width
    part = part.reshape(chips * tiles, lines, strip_width) * jnp.exp2(-exponents[16:17])
    tail = jnp.broadcast_to(exponents[16:24], (chips * tiles, 8, strip_width))
    part = jnp.concatenate([part, tail], axis=1).astype(jnp.float16)
    members = [
        [(2 * chip + side) * tiles + tile for chip in range(chips) for tile in range(tiles)]
        for side in range(2)
    ]
    part = lax.all_to_all(
        part, ("group", "tile"), 0, 0, axis_index_groups=members, tiled=True
    )
    part = jnp.sum(
        part[:, :lines].astype(F32) * jnp.exp2(part[:, lines : lines + 1].astype(F32)), axis=0
    )
    probe_squares = jnp.sum(part * part)

    def scale_of(rim, at):
        row = row_count + 8 * at
        return jnp.exp2(rim[:, row : row + 1].astype(F32))

    def widened(rim):
        return rim[:, :row_count].astype(F32)

    own_second = (
        own_second
        + widened(second_from_right) * scale_of(second_from_right, 0)
        + widened(from_left[2:]) * scale_of(from_left[2:], 0)
    )
    own_first = (
        own_first
        + widened(first_from_right) * scale_of(second_from_right, 1)
        + widened(from_left[:2]) * scale_of(from_left[:2], 1)
    )
    own_grad = jnp.concatenate([own_first, own_second])
    object_squares = jnp.sum(own_grad * own_grad)
    totals = summed(lane_row([object_squares, probe_squares]))
    object_total, probe_total = totals[0], totals[1]
    object_count = 4 * row_count * strip_width * groups * tiles
    object_factor = object_step / jnp.sqrt(object_total / object_count + epsilon)
    object_new = object_slices.astype(F32) - object_factor * own_grad

    part = part.reshape(piece, size)
    for bit in (1, 2):
        other = swapped(part, "group", bit)
        mine = (lax.axis_index("group") // bit) % 2
        part = jnp.where(mine == 0, jnp.concatenate([part, other]), jnp.concatenate([other, part]))
    probe_factor = probe_step / jnp.sqrt(probe_total / probe.size + epsilon)
    start_row = lax.axis_index("tile") * share
    probe_rows = lax.dynamic_slice_in_dim(probe, start_row, share, 0)
    probe_new = probe_rows - probe_factor * part
    return (object_new, probe_new)


def solution(mesh):
    return jax.shard_map(
        shards,
        mesh=mesh,
        in_specs=(
            P(None, "group", "tile"),
            P(),
            P("group", "tile", None, None, None, None, None),
            P("group", "tile", None, None, None),
            P("group", "tile", None),
            P("group", "tile", None),
        ),
        out_specs=(P(None, "group", "tile"), P("tile", None)),
        check_vma=False,
    )
```
